256 devices in a mesh: tok: 32 (over y_hi, z, core), col: 8 (over x, y_lo).
Axes of the slice: x: 4, y: 4 (y_hi: 2, y_lo: 2; y = y_hi * 2 + y_lo), z: 8, core: 2. Of those that a mesh axis runs over, the one named last changes fastest.
Arguments:
- activations: bfloat16 [32768, 4096], P('tok'), may hold values from -14 to 14
- targets: bfloat16 [32768, 4096], P('tok', 'col'), may hold values from -20 to 20
- map_weight: float32 [4096, 4096], P('tok', 'col'), may hold values from -1 to 2
- first_moment: float32 [4096, 4096], P('tok', 'col'), may hold values from -0.12 to 0.12
- second_moment: float32 [4096, 4096], P('tok', 'col'), may hold values from 0.0001 to 0.001
- down_weight: bfloat16 [14336, 4096], P('tok', 'col'), may hold values from -6 to 6
Outputs:
- new_map: float32 [4096, 4096], P('tok', 'col')
- joined: bfloat16 [14336, 4096], P('tok', 'col')
The draws below stay inside these ranges and needn't reach their ends.
All inputs are finite; a program needn't handle non-finite values.
Results may differ from the reference program's by a relative error of at most 0.0041.
The reference program's roundings to bfloat16 on the way (of `map_half` and `d_pred`) count: a program that leaves them out, or rounds other values in their place, can miss the bound.
Values may be sent and summed in bfloat16 or wider, within the bound.
No kernel may reach another device: no remote copies, remote signals or barrier semaphores. Data moves between devices by JAX's collectives and lax.ppermute only.
A program may use at most 128 MiB of HBM per device.

```python
import math
import jax
import jax.numpy as jnp
from jax import lax

D = 4096
FF = 14336
TOKENS = 32768


def token_fields(key):
    base_key = jax.random.fold_in(key, 7)
    noise_key = jax.random.fold_in(key, 11)
    base = jax.random.truncated_normal(base_key, -4.0, 4.0, (TOKENS, D), jnp.float32)
    noise = jax.random.truncated_normal(noise_key, -4.0, 4.0, (TOKENS, D), jnp.float32)
    inputs = base
    outputs = 0.7 * base + 0.7 * noise
    return (inputs, outputs)


def draw_activations(key, part):
    inputs, outputs = token_fields(key)
    return inputs.astype(jnp.bfloat16)


def draw_targets(key, part):
    inputs, outputs = token_fields(key)
    return outputs.astype(jnp.bfloat16)


def draw_map_weight(key, part):
    noise_key = jax.random.fold_in(key, 23)
    spread = 1.0 / jnp.sqrt(jnp.float32(D))
    noise = jax.random.truncated_normal(noise_key, -4.0, 4.0, (D, D), jnp.float32) * spread
    return (jnp.eye(D, dtype=jnp.float32) + noise).astype(jnp.float32)


def shard_levels(key, dims, pieces, least, largest):
    factor_of, own = 1.0, jax.random.fold_in(key, 6)
    for position, shards_of in pieces:
        draws = jnp.exp(jax.random.uniform(jax.random.fold_in(own, position), (shards_of,), jnp.float32, least / len(pieces), largest / len(pieces)))
        factor_of = factor_of * jnp.repeat(draws, dims[position] // shards_of).reshape([-1 if axis == position else 1 for axis in range(len(dims))])
    return factor_of


def normal_values(own_key, extent, deviation, most, split=(), kind=jnp.bfloat16):
    drawn = deviation * jax.random.normal(own_key, extent, jnp.float32)
    if split:
        drawn = drawn * shard_levels(own_key, extent, split, -0.22, 0.18)
    return jnp.clip(drawn, -most, most).astype(kind)


def setup_inputs(seed: int = 0) -> dict:
    keys = jax.random.split(jax.random.key(seed), 7)
    return {
        "activations": draw_activations(jax.random.fold_in(keys[6], 71), 0),
        "targets": draw_targets(jax.random.fold_in(keys[6], 71), 0),
        "map_weight": draw_map_weight(jax.random.fold_in(keys[6], 71), 0),
        "first_moment": normal_values(keys[3], (D, D), 0.02, 0.12, ((0, 32), (1, 8)), jnp.float32),
        "second_moment": jnp.clip(jnp.exp(math.log(0.001) - 2.3025852 * jax.random.uniform(keys[4], (D, D), jnp.float32) ** shard_levels(keys[4], (D, D), ((0, 32), (1, 8)), -0.2, 0.2)), 0.0001, 0.001),
        "down_weight": normal_values(keys[5], (FF, D), 1.0, 6.0, ((0, 32), (1, 8))),
    }


def reference(activations, targets, map_weight, first_moment, second_moment, down_weight):
    high = lax.Precision.HIGHEST
    map_half = map_weight.astype(jnp.bfloat16)
    inputs = activations.astype(jnp.float32)
    predicted = jnp.dot(inputs, map_half.astype(jnp.float32), precision=high)
    target32 = targets.astype(jnp.float32)
    inner = lax.optimization_barrier(jnp.sum(predicted * target32, axis=1))
    pred_sq = lax.optimization_barrier(jnp.sum(predicted * predicted, axis=1))
    target_sq = lax.optimization_barrier(jnp.sum(target32 * target32, axis=1))
    pred_norm = jnp.sqrt(pred_sq + 1e-06)
    targ_norm = jnp.sqrt(target_sq + 1e-06)
    scale = 1.0 / (pred_norm * targ_norm)
    coef = inner * scale / (pred_norm * pred_norm)
    d_pred = (coef[:, None] * predicted - scale[:, None] * target32).astype(jnp.bfloat16)
    grad = jnp.dot(inputs.T, d_pred.astype(jnp.float32), precision=high)
    moment1 = 0.9 * first_moment + 0.1 * grad
    moment2 = 0.95 * second_moment + 0.05 * grad * grad
    new_map = map_weight - 0.02 * (moment1 / (1.0 - 0.9 ** 10)) / (jnp.sqrt(moment2 / (1.0 - 0.95 ** 10)) + 1e-08)
    joined = jnp.dot(down_weight.astype(jnp.float32), new_map.astype(jnp.bfloat16).astype(jnp.float32), precision=high)
    return (new_map, joined.astype(jnp.bfloat16))
```

```python
import jax
import jax.numpy as jnp
from jax import lax
from jax.sharding import Mesh
from jax.sharding import PartitionSpec as P

COL = ("x", "yl")
TOK = ("yh", "z", "core")
NZ = 8
HALF = 256
SWAP = [(0, 1), (1, 0)]


def swap(x, axis):
    return lax.ppermute(x, axis, SWAP)


def shift(x, axis, by):
    n = lax.axis_size(axis)
    return lax.ppermute(x, axis, [(i, (i + by) % n) for i in range(n)])


def after(x, *deps):
    return lax.optimization_barrier((x, *deps))[0]


def halves(x, core):
    mine = lax.dynamic_slice_in_dim(x, core * HALF, HALF, 1)
    theirs = lax.dynamic_slice_in_dim(x, (1 - core) * HALF, HALF, 1)
    return mine, theirs


def ordered(mine, theirs, index, axis):
    first = jnp.where(index == 0, mine, theirs)
    second = jnp.where(index == 0, theirs, mine)
    return jnp.concatenate([first, second], axis)


def ring_gather(block, use):
    z = lax.axis_index("z")
    up = down = block
    for step in range(1, 5):
        last_up, last_down = up, down
        up = shift(last_up, "z", 1)
        if step < 4:
            down = shift(last_down, "z", -1)
        if step == 1:
            use(block, z)
        use(up, (z - step) % NZ)
        if step < 4:
            use(down, (z + step) % NZ)


def columns(x, start):
    return lax.dynamic_slice_in_dim(x, start, 256, 1)


def adam_step(weight, first, second, grad):
    moment1 = 0.9 * first + 0.1 * grad
    moment2 = 0.95 * second + 0.05 * grad * grad
    return weight - 0.02 * (moment1 / (1.0 - 0.9**10)) / (
        jnp.sqrt(moment2 / (1.0 - 0.95**10)) + 1e-08
    )


def per_device(activations, targets, map_weight, first_moment, second_moment, down_weight):
    core = lax.axis_index("core")
    z = lax.axis_index("z")
    yh = lax.axis_index("yh")

    mine, theirs = halves(map_weight.astype(jnp.bfloat16), core)
    chip_map = ordered(mine, swap(theirs, "core"), core, 0)
    other_map = swap(chip_map, "yh")
    block = ordered(chip_map, other_map, yh, 0)

    acts = (activations, swap(activations, "core"))
    mine, theirs = halves(targets, core)
    targs = tuple(t.astype(jnp.float32) for t in (mine, swap(theirs, "core")))

    predicted = [None, None]

    def add_predicted(blk, at):
        for i in range(2):
            for half in range(2):
                part = jnp.dot(
                    columns(acts[i], half * 2048 + at * 256),
                    blk[half * 256 : half * 256 + 256],
                    preferred_element_type=jnp.float32,
                )
                predicted[i] = part if predicted[i] is None else predicted[i] + part

    ring_gather(block, add_predicted)

    down = after(down_weight, other_map)
    pair = ordered(down, swap(down, "yl"), lax.axis_index("yl"), 1)
    x = lax.axis_index("x")
    full = jnp.zeros((down.shape[0], 4096), jnp.bfloat16)
    full = lax.dynamic_update_slice_in_dim(full, pair, x * 1024, 1)
    for by in range(1, 4):
        full = lax.dynamic_update_slice_in_dim(
            full, shift(pair, "x", by), ((x - by) % 4) * 1024, 1
        )
    downs = (full, swap(full, "core"))

    def sums(i):
        return jnp.stack(
            [
                jnp.sum(predicted[i] * targs[i], axis=1),
                jnp.sum(predicted[i] * predicted[i], axis=1),
                jnp.sum(targs[i] * targs[i], axis=1),
            ]
        )

    total = sums(0) + swap(sums(1), "core")
    copies = jnp.broadcast_to(total.reshape(1, 1, -1), (8, 1, total.size))
    total = jnp.sum(lax.all_to_all(copies, COL, 0, 0, tiled=True), axis=0).reshape(total.shape)
    inner, pred_sq, target_sq = total
    pred_norm = jnp.sqrt(pred_sq + 1e-06)
    targ_norm = jnp.sqrt(target_sq + 1e-06)
    scale = 1.0 / (pred_norm * targ_norm)
    coef = inner * scale / (pred_norm * pred_norm)
    own = jnp.stack([coef, scale])
    factors = (own, swap(own, "core"))
    d_pred = [
        (f[0][:, None] * p - f[1][:, None] * t).astype(jnp.bfloat16)
        for f, p, t in zip(factors, predicted, targs)
    ]

    def grad_block(at):
        at = at % NZ
        parts = []
        for half in range(2):
            part = sum(
                lax.dot_general(
                    columns(acts[i], half * 2048 + at * 256),
                    d_pred[i],
                    (((0,), (0,)), ((), ())),
                    preferred_element_type=jnp.float32,
                )
                for i in range(2)
            )
            parts.append(part)
        return lax.optimization_barrier(jnp.concatenate(parts, 0))

    up = down_ = None
    for step in range(4):
        block_up = grad_block(z + 4 - step)
        sent_up = block_up if up is None else block_up + up.astype(jnp.float32)
        up = shift(sent_up.astype(jnp.bfloat16), "z", 1)
        if step < 3:
            block_down = grad_block(z - 3 + step)
            sent_down = block_down if down_ is None else block_down + down_.astype(jnp.float32)
            down_ = shift(sent_down.astype(jnp.bfloat16), "z", -1)
    own = grad_block(z) + down_.astype(jnp.float32)
    own = own + up.astype(jnp.float32)
    mine = lax.dynamic_slice_in_dim(own, yh * 256, 256, 0)
    theirs = lax.dynamic_slice_in_dim(own, (1 - yh) * 256, 256, 0)
    grad = mine + swap(theirs.astype(jnp.bfloat16), "yh").astype(jnp.float32)

    def chip_rows(a):
        mine, theirs = halves(a, core)
        return ordered(mine, swap(theirs, "core"), core, 0)

    new_chip = adam_step(
        chip_rows(map_weight), chip_rows(first_moment), chip_rows(second_moment), grad
    )
    new_half = new_chip.astype(jnp.bfloat16)
    block = ordered(new_half, swap(new_half, "yh"), yh, 0)
    rows_mine = lax.dynamic_slice_in_dim(new_chip, core * 128, 128, 0)
    rows_theirs = lax.dynamic_slice_in_dim(new_chip, (1 - core) * 128, 128, 0)
    new_map = ordered(rows_mine, swap(rows_theirs, "core"), core, 1)

    joined = [None, None]

    def add_joined(blk, at):
        for i in range(2):
            for half in range(2):
                part = jnp.dot(
                    columns(downs[i], half * 2048 + at * 256),
                    blk[half * 256 : half * 256 + 256],
                    preferred_element_type=jnp.float32,
                )
                joined[i] = part if joined[i] is None else joined[i] + part

    ring_gather(block, add_joined)
    joined = [j.astype(jnp.bfloat16) for j in joined]
    joined = ordered(joined[0], swap(joined[1], "core"), core, 1)
    return (new_map, joined)


def solution(mesh):
    split = Mesh(mesh.devices.reshape(2, 8, 2, 4, 2), ("yh", "z", "core", "x", "yl"))
    return jax.shard_map(
        per_device,
        mesh=split,
        in_specs=(P(TOK, None), P(TOK, COL), P(TOK, COL), P(TOK, COL), P(TOK, COL), P(TOK, COL)),
        out_specs=(P(TOK, COL), P(TOK, COL)),
        check_vma=False,
    )
```

```python
import functools

import jax
import jax.numpy as jnp
from jax import lax
from jax.experimental import pallas as pl
from jax.experimental.pallas import tpu as pltpu
from jax.sharding import Mesh
from jax.sharding import PartitionSpec as P

COL = ("x", "yl")
TOK = ("yh", "z", "core")
NZ = 8
HALF = 256
VMEM_LIMIT = 2 * 2**20
SWAP = [(0, 1), (1, 0)]


def swap(x, axis):
    return lax.ppermute(x, axis, SWAP)


def shift(x, axis, by):
    n = lax.axis_size(axis)
    return lax.ppermute(x, axis, [(i, (i + by) % n) for i in range(n)])


def after(x, *deps):
    return lax.optimization_barrier((x, *deps))[0]


def halves(x, index, axis):
    first, second = jnp.split(x, 2, axis)
    return jnp.where(index, second, first), jnp.where(index, first, second)


def ordered(mine, theirs, index, axis):
    first = jnp.where(index, theirs, mine)
    second = jnp.where(index, mine, theirs)
    return jnp.concatenate([first, second], axis)


def multiply_kernel(offsets, summed, rowsums, tile, table, *refs):
    refs = list(refs)
    count = len(offsets)
    mats = [refs.pop(0) for _ in range(2)]
    blocks = [refs.pop(0) for _ in range(count)]
    sums = [refs.pop(0) for _ in range(2)] if summed else None
    targets = [refs.pop(0) for _ in range(2)] if rowsums else None
    outs = [refs.pop(0) for _ in range(2)]

    def step(s, carry):
        at = pl.ds(pl.multiple_of(s * tile, tile), tile)
        rows = []
        for i in range(2):
            total = sums[i][at, :] if summed else None
            for b in range(count):
                for h in range(2):
                    column = pl.multiple_of((h * NZ + table[offsets[b]]) * 256, 256)
                    part = jnp.dot(
                        mats[i][at, pl.ds(column, 256)],
                        blocks[b][h * 256 : h * 256 + 256, :],
                        preferred_element_type=jnp.float32,
                    )
                    total = part if total is None else total + part
            outs[i][at, :] = total.astype(outs[i].dtype)
            if rowsums:
                target = targets[i][at, :].astype(jnp.float32)
                rows += [
                    jnp.sum(value, axis=1, keepdims=True)
                    for value in (total * target, total * total, target * target)
                ]
        if rowsums:
            shape = (tile, 128)
            place = lax.broadcasted_iota(jnp.int32, shape, 1)
            result = jnp.zeros(shape, jnp.float32)
            for lane, row in zip((0, 1, 2, 4, 5, 6), rows):
                result = jnp.where(place == lane, row, result)
            refs[0][:, at] = result.T[:8]
        return carry

    lax.fori_loop(0, outs[0].shape[0] // tile, step, 0)


def load_kernel(source, target, sem):
    copy = pltpu.make_async_copy(source, target, sem)
    copy.start()
    copy.wait()


def load(x):
    return pl.pallas_call(
        load_kernel,
        in_specs=[pl.BlockSpec(memory_space=pltpu.HBM)],
        out_specs=pl.BlockSpec(memory_space=pltpu.VMEM),
        out_shape=jax.ShapeDtypeStruct(x.shape, x.dtype),
        scratch_shapes=[pltpu.SemaphoreType.DMA],
        compiler_params=pltpu.CompilerParams(vmem_limit_bytes=VMEM_LIMIT),
        name="load",
    )(x)


def assemble_kernel(table, *refs):
    parts, target, sems = refs[:4], refs[4], refs[5]
    x = table[NZ]
    copies = []
    for by in range(4):
        column = pl.multiple_of(((x + 4 - by) % 4) * 1024, 1024)
        copies.append(
            pltpu.make_async_copy(parts[by], target.at[:, pl.ds(column, 1024)], sems.at[by])
        )
    for copy in copies:
        copy.start()
    for copy in copies:
        copy.wait()


def assemble(table, parts):
    return pl.pallas_call(
        assemble_kernel,
        in_specs=[pl.BlockSpec(memory_space=pltpu.SMEM)]
        + [pl.BlockSpec(memory_space=pltpu.HBM)] * 4,
        out_specs=pl.BlockSpec(memory_space=pltpu.VMEM),
        out_shape=jax.ShapeDtypeStruct((parts[0].shape[0], 4096), parts[0].dtype),
        scratch_shapes=[pltpu.SemaphoreType.DMA((4,))],
        compiler_params=pltpu.CompilerParams(vmem_limit_bytes=5 * VMEM_LIMIT),
        name="assemble",
    )(table, *parts)


def in_vmem(count):
    return [pl.BlockSpec(memory_space=pltpu.VMEM)] * count


def multiply(table, mats, blocks, offsets, sums=None, targets=None, dtype=jnp.float32):
    m = mats[0].shape[0]
    tile = 256 if m % 256 == 0 else 224
    count = len(blocks)
    args = [*mats, *blocks, *(sums or []), *(targets or [])]
    out_shape = [jax.ShapeDtypeStruct((m, HALF), dtype)] * 2
    if targets is not None:
        out_shape = out_shape + [jax.ShapeDtypeStruct((8, m), jnp.float32)]
    return pl.pallas_call(
        functools.partial(
            multiply_kernel, offsets, sums is not None, targets is not None, tile
        ),
        in_specs=[pl.BlockSpec(memory_space=pltpu.SMEM)] + in_vmem(len(args)),
        out_specs=in_vmem(len(out_shape)),
        out_shape=out_shape,
        compiler_params=pltpu.CompilerParams(
            vmem_limit_bytes=VMEM_LIMIT if m == 1024 else 5 * VMEM_LIMIT
        ),
        cost_estimate=pl.CostEstimate(
            flops=4 * m * HALF * 512 * count,
            bytes_accessed=4 * m * 512 * count + 8 * m * HALF,
            transcendentals=0,
        ),
        name=f"multiply_{m}_{count}",
    )(table, *args)


def grad_kernel(offset, table, *refs):
    mats, grads, out = refs[0:2], refs[2:4], refs[4]
    for h in range(2):
        column = pl.multiple_of((h * NZ + table[offset]) * 256, 256)
        part = None
        for i in range(2):
            p = lax.dot_general(
                mats[i][:, pl.ds(column, 256)],
                grads[i][...],
                (((0,), (0,)), ((), ())),
                preferred_element_type=jnp.float32,
            )
            part = p if part is None else part + p
        out[h * 256 : h * 256 + 256, :] = part


def grad_block(table, mats, grads, offset):
    m = mats[0].shape[0]
    return pl.pallas_call(
        functools.partial(grad_kernel, offset % NZ),
        in_specs=[pl.BlockSpec(memory_space=pltpu.SMEM)] + in_vmem(4),
        out_specs=pl.BlockSpec(memory_space=pltpu.VMEM),
        out_shape=jax.ShapeDtypeStruct((512, HALF), jnp.float32),
        compiler_params=pltpu.CompilerParams(vmem_limit_bytes=VMEM_LIMIT),
        cost_estimate=pl.CostEstimate(
            flops=4 * m * HALF * 512, bytes_accessed=4 * m * 512, transcendentals=0
        ),
        name="grad_block",
    )(table, *mats, *grads)


def ring_multiply(table, block, mats, targets=None, dtype=jnp.float32):
    up = down = block
    sums = None
    ready = [(block, 0)]
    for step in range(4):
        if sums is not None:
            up, sums = lax.optimization_barrier((up, sums))
        if step > 0:
            ready += [(up, NZ - step), (down, step)]
        up = shift(up, "z", 1)
        if step < 3:
            down = shift(down, "z", -1)
        if step > 0:
            blocks, offsets = zip(*ready)
            sums = list(multiply(table, mats, blocks, offsets, sums))
            ready = []
    return multiply(table, mats, [up], [4], sums, targets, dtype)


def adam_step(weight, first, second, grad):
    moment1 = 0.9 * first + 0.1 * grad
    moment2 = 0.95 * second + 0.05 * grad * grad
    return weight - 0.02 * (moment1 / (1.0 - 0.9**10)) / (
        jnp.sqrt(moment2 / (1.0 - 0.95**10)) + 1e-08
    )


def per_device(activations, targets, map_weight, first_moment, second_moment, down_weight):
    core, yh, yl = (lax.axis_index(a) == 1 for a in ("core", "yh", "yl"))
    z = lax.axis_index("z").astype(jnp.int32)
    x = lax.axis_index("x").astype(jnp.int32)
    steps = lax.iota(jnp.int32, NZ + 1)
    table = jnp.where(steps < NZ, jnp.bitwise_and(z + steps, NZ - 1), x)

    map_half, yh, yl, table = lax.optimization_barrier(
        (map_weight.astype(jnp.bfloat16), yh, yl, table)
    )
    mine, theirs = halves(map_half, core, 1)
    chip_map = ordered(mine, swap(theirs, "core"), core, 0)
    other_map = swap(chip_map, "yh")
    block = ordered(chip_map, other_map, yh, 0)

    partner = swap(after(activations, chip_map), "core")
    acts = [activations, load(partner)]
    mine, theirs = halves(after(targets, other_map), core, 1)
    targs = [mine, swap(theirs, "core")]

    *predicted, total = ring_multiply(table, block, acts, targs)

    down = after(down_weight, other_map)
    pair = ordered(down, swap(down, "yl"), yl, 1)

    theirs = swap(total, "core")
    total = total + jnp.concatenate([theirs[4:], theirs[:4]], 0)
    total = total + swap(total, "yl")
    total = total + shift(total, "x", 1) + shift(total, "x", 2) + shift(total, "x", 3)
    d_pred = []
    for i in range(2):
        inner, pred_sq, target_sq = total[4 * i], total[4 * i + 1], total[4 * i + 2]
        pred_norm = jnp.sqrt(pred_sq + 1e-06)
        targ_norm = jnp.sqrt(target_sq + 1e-06)
        scale = 1.0 / (pred_norm * targ_norm)
        coef = inner * scale / (pred_norm * pred_norm)
        d_pred.append(
            (
                coef[:, None] * predicted[i] - scale[:, None] * targs[i].astype(jnp.float32)
            ).astype(jnp.bfloat16)
        )

    up = down_ = None
    sent = d_pred[0]
    for step in range(4):
        grads = [after(d_pred[0], sent), d_pred[1]]
        part = grad_block(table, acts, grads, 4 - step)
        sent = part if up is None else part + up.astype(jnp.float32)
        sent = sent.astype(jnp.bfloat16)
        up = shift(sent, "z", 1)
        if step < 3:
            grads = [after(d_pred[0], sent), d_pred[1]]
            part = grad_block(table, acts, grads, step - 3)
            sent = part if down_ is None else part + down_.astype(jnp.float32)
            sent = sent.astype(jnp.bfloat16)
            down_ = shift(sent, "z", -1)
        if step == 0:
            pair = after(pair, sent)
            parts = [pair] + [shift(pair, "x", by) for by in range(1, 4)]
    own = grad_block(table, acts, [after(d_pred[0], sent), d_pred[1]], 0)
    own = own + down_.astype(jnp.float32) + up.astype(jnp.float32)
    full = assemble(table, lax.optimization_barrier((*parts, own))[:4])
    downs = [full, swap(full, "core")]
    mine, theirs = halves(own, yh, 0)
    grad = mine + swap(theirs.astype(jnp.bfloat16), "yh").astype(jnp.float32)

    state = jnp.concatenate([map_weight, first_moment, second_moment], 0)
    mine, theirs = halves(after(state, block), core, 1)
    pieces = zip(jnp.split(mine, 3, 0), jnp.split(swap(theirs, "core"), 3, 0))
    new_chip = adam_step(*(ordered(a, b, core, 0) for a, b in pieces), grad)
    new_half = new_chip.astype(jnp.bfloat16)
    block = ordered(new_half, swap(new_half, "yh"), yh, 0)
    rows_mine, rows_theirs = halves(new_chip, core, 0)
    new_map = ordered(rows_mine, swap(rows_theirs, "core"), core, 1)

    joined = ring_multiply(table, block, downs, dtype=jnp.bfloat16)
    joined = ordered(joined[0], swap(joined[1], "core"), core, 1)
    return (new_map, joined)


def solution(mesh):
    split = Mesh(mesh.devices.reshape(2, 8, 2, 4, 2), ("yh", "z", "core", "x", "yl"))
    return jax.shard_map(
        per_device,
        mesh=split,
        in_specs=(P(TOK, None), P(TOK, COL), P(TOK, COL), P(TOK, COL), P(TOK, COL), P(TOK, COL)),
        out_specs=(P(TOK, COL), P(TOK, COL)),
        check_vma=False,
    )
```

```python
import functools

import jax
import jax.numpy as jnp
from jax import lax
from jax.experimental import pallas as pl
from jax.experimental.pallas import tpu as pltpu
from jax.sharding import Mesh
from jax.sharding import PartitionSpec as P

COL = ("x", "yl")
TOK = ("yh", "z", "core")
NZ = 8
HALF = 256
VMEM_LIMIT = 2 * 2**20
SWAP = [(0, 1), (1, 0)]


def swap(x, axis):
    return lax.ppermute(x, axis, SWAP)


def shift(x, axis, by):
    n = lax.axis_size(axis)
    return lax.ppermute(x, axis, [(i, (i + by) % n) for i in range(n)])


def after(x, *deps):
    return lax.optimization_barrier((x, *deps))[0]


def halves(x, index, axis):
    first, second = jnp.split(x, 2, axis)
    return jnp.where(index, second, first), jnp.where(index, first, second)


def ordered(mine, theirs, index, axis):
    first = jnp.where(index, theirs, mine)
    second = jnp.where(index, mine, theirs)
    return jnp.concatenate([first, second], axis)


def multiply_kernel(offsets, summed, rowsums, tile, table, *refs):
    refs = list(refs)
    count = len(offsets)
    mats = [refs.pop(0) for _ in range(2)]
    blocks = [refs.pop(0) for _ in range(count)]
    sums = [refs.pop(0) for _ in range(2)] if summed else None
    targets = [refs.pop(0) for _ in range(2)] if rowsums else None
    outs = [refs.pop(0) for _ in range(2)]

    def step(s, carry):
        at = pl.ds(pl.multiple_of(s * tile, tile), tile)
        rows = []
        for i in range(2):
            total = sums[i][at, :] if summed else None
            for b in range(count):
                for h in range(2):
                    column = pl.multiple_of((h * NZ + table[offsets[b]]) * 256, 256)
                    part = jnp.dot(
                        mats[i][at, pl.ds(column, 256)],
                        blocks[b][h * 256 : h * 256 + 256, :],
                        preferred_element_type=jnp.float32,
                    )
                    total = part if total is None else total + part
            outs[i][at, :] = total.astype(outs[i].dtype)
            if rowsums:
                target = targets[i][at, :].astype(jnp.float32)
                rows += [
                    jnp.sum(value, axis=1, keepdims=True)
                    for value in (total * target, total * total, target * target)
                ]
        if rowsums:
            shape = (tile, 128)
            place = lax.broadcasted_iota(jnp.int32, shape, 1)
            result = jnp.zeros(shape, jnp.float32)
            for lane, row in zip((0, 1, 2, 4, 5, 6), rows):
                result = jnp.where(place == lane, row, result)
            refs[0][:, at] = result.T[:8]
        return carry

    lax.fori_loop(0, outs[0].shape[0] // tile, step, 0)


def load_kernel(source, target, sem):
    copy = pltpu.make_async_copy(source, target, sem)
    copy.start()
    copy.wait()


def load(x):
    return pl.pallas_call(
        load_kernel,
        in_specs=[pl.BlockSpec(memory_space=pltpu.HBM)],
        out_specs=pl.BlockSpec(memory_space=pltpu.VMEM),
        out_shape=jax.ShapeDtypeStruct(x.shape, x.dtype),
        scratch_shapes=[pltpu.SemaphoreType.DMA],
        compiler_params=pltpu.CompilerParams(vmem_limit_bytes=VMEM_LIMIT),
        name="load",
    )(x)


PARTS = ((0, 0, 1024), (3, 0, 1024), (1, 0, 1024), (2, 0, 512), (2, 512, 512))


def assemble_kernel(table, *refs):
    parts, target, sems = refs[:5], refs[5], refs[6]
    copies = []
    for at, (by, first, width) in enumerate(PARTS):
        column = pl.multiple_of((table[NZ] + by) % 4 * 1024 + first, 512)
        copies.append(
            pltpu.make_async_copy(parts[at], target.at[:, pl.ds(column, width)], sems.at[at])
        )
    for copy in copies:
        copy.start()
    for copy in copies:
        copy.wait()


def assemble(table, parts):
    return pl.pallas_call(
        assemble_kernel,
        in_specs=[pl.BlockSpec(memory_space=pltpu.SMEM)]
        + [pl.BlockSpec(memory_space=pltpu.HBM)] * 5,
        out_specs=pl.BlockSpec(memory_space=pltpu.VMEM),
        out_shape=jax.ShapeDtypeStruct((parts[0].shape[0], 4096), parts[0].dtype),
        scratch_shapes=[pltpu.SemaphoreType.DMA((5,))],
        compiler_params=pltpu.CompilerParams(vmem_limit_bytes=5 * VMEM_LIMIT),
        name="assemble",
    )(table, *parts)


def in_vmem(count):
    return [pl.BlockSpec(memory_space=pltpu.VMEM)] * count


def multiply(table, mats, blocks, offsets, sums=None, targets=None, dtype=jnp.float32):
    m = mats[0].shape[0]
    tile = 256 if m % 256 == 0 else 224
    count = len(blocks)
    args = [*mats, *blocks, *(sums or []), *(targets or [])]
    out_shape = [jax.ShapeDtypeStruct((m, HALF), dtype)] * 2
    if targets is not None:
        out_shape = out_shape + [jax.ShapeDtypeStruct((8, m), jnp.float32)]
    return pl.pallas_call(
        functools.partial(
            multiply_kernel, offsets, sums is not None, targets is not None, tile
        ),
        in_specs=[pl.BlockSpec(memory_space=pltpu.SMEM)] + in_vmem(len(args)),
        out_specs=in_vmem(len(out_shape)),
        out_shape=out_shape,
        compiler_params=pltpu.CompilerParams(
            vmem_limit_bytes=VMEM_LIMIT if m == 1024 else 5 * VMEM_LIMIT
        ),
        cost_estimate=pl.CostEstimate(
            flops=4 * m * HALF * 512 * count,
            bytes_accessed=4 * m * 512 * count + 8 * m * HALF,
            transcendentals=0,
        ),
        name=f"multiply_{m}_{count}",
    )(table, *args)


def grad_kernel(offset, table, *refs):
    mats, grads, out = refs[0:2], refs[2:4], refs[4]

    def step(h, carry):
        column = pl.multiple_of((h * NZ + table[offset]) * 256, 256)
        part = None
        for i in range(2):
            p = lax.dot_general(
                mats[i][:, pl.ds(column, 256)],
                grads[i][...],
                (((0,), (0,)), ((), ())),
                preferred_element_type=jnp.float32,
            )
            part = p if part is None else part + p
        out[pl.ds(pl.multiple_of(h * 256, 256), 256), :] = part.astype(out.dtype)
        return carry

    lax.fori_loop(0, 2, step, 0)


def grad_block(table, mats, grads, offset, dtype=jnp.float32):
    m = mats[0].shape[0]
    return pl.pallas_call(
        functools.partial(grad_kernel, offset % NZ),
        in_specs=[pl.BlockSpec(memory_space=pltpu.SMEM)] + in_vmem(4),
        out_specs=pl.BlockSpec(memory_space=pltpu.VMEM),
        out_shape=jax.ShapeDtypeStruct((512, HALF), dtype),
        compiler_params=pltpu.CompilerParams(vmem_limit_bytes=VMEM_LIMIT),
        cost_estimate=pl.CostEstimate(
            flops=4 * m * HALF * 512, bytes_accessed=4 * m * 512, transcendentals=0
        ),
        name="grad_block",
    )(table, *mats, *grads)


def ring_multiply(table, block, mats, targets=None, dtype=jnp.float32, early=None, later=None):
    up = down = block
    sums = None
    ready = [(block, 0)]
    for step in range(4):
        if sums is not None:
            up, sums = lax.optimization_barrier((up, sums))
        if step == 2 and early is not None:
            up, early = lax.optimization_barrier((up, early))
        if step > 0:
            ready += [(up, NZ - step), (down, step)]
        up = shift(up, "z", 1)
        if step < 3:
            down = shift(down, "z", -1)
        if step > 0:
            blocks, offsets = zip(*ready)
            sums = list(multiply(table, mats, blocks, offsets, sums))
            ready = []
    if later is not None:
        up, later = lax.optimization_barrier((up, later))
    return *multiply(table, mats, [up], [4], sums, targets, dtype), later


def adam_step(weight, first, second, grad):
    moment1 = 0.9 * first + 0.1 * grad
    moment2 = 0.95 * second + 0.05 * grad * grad
    return weight - 0.02 * (moment1 / (1.0 - 0.9**10)) / (
        jnp.sqrt(moment2 / (1.0 - 0.95**10)) + 1e-08
    )


def per_device(activations, targets, map_weight, first_moment, second_moment, down_weight):
    core, yh, yl = (lax.axis_index(a) == 1 for a in ("core", "yh", "yl"))
    z = lax.axis_index("z").astype(jnp.int32)
    x = lax.axis_index("x").astype(jnp.int32)
    steps = lax.iota(jnp.int32, NZ + 1)
    table = jnp.where(steps < NZ, jnp.bitwise_and(z + steps, NZ - 1), x)

    map_half, yh, yl, table = lax.optimization_barrier(
        (map_weight.astype(jnp.bfloat16), yh, yl, table)
    )
    mine, theirs = halves(map_half, core, 1)
    chip_map = ordered(mine, swap(theirs, "core"), core, 0)
    other_map = swap(chip_map, "yh")
    block = ordered(chip_map, other_map, yh, 0)

    partner = swap(after(activations, chip_map), "core")
    acts = [activations, load(partner)]
    mine, theirs = halves(after(targets, other_map), core, 1)
    targs = [mine, swap(theirs, "core")]

    down = after(down_weight, other_map)
    pair = ordered(down, swap(down, "yl"), yl, 1)

    right, left = shift(pair, "x", 1), shift(pair, "x", -1)

    state = jnp.concatenate([map_weight, first_moment, second_moment], 0)
    mine, theirs = halves(after(state, block), core, 1)
    pieces = zip(jnp.split(mine, 3, 0), jnp.split(swap(theirs, "core"), 3, 0))
    state = jnp.concatenate([ordered(a, b, core, 0) for a, b in pieces], 0)
    other_state = swap(state, "yh")

    *predicted, total, moved = ring_multiply(
        table, block, acts, targs, early=pair, later=(right, left, other_state)
    )
    right, left, other_state = moved
    far = [shift(right[:, :512], "x", 1), shift(left[:, 512:], "x", -1)]

    theirs = swap(total, "core")
    total = total + jnp.concatenate([theirs[4:], theirs[:4]], 0)
    total = total + swap(total, "yl")
    total = total + lax.ppermute(total, "x", [(0, 1), (1, 0), (2, 3), (3, 2)])
    total = total + shift(total, "x", 2)
    d_pred = []
    for i in range(2):
        inner, pred_sq, target_sq = total[4 * i], total[4 * i + 1], total[4 * i + 2]
        pred_norm = jnp.sqrt(pred_sq + 1e-06)
        targ_norm = jnp.sqrt(target_sq + 1e-06)
        scale = 1.0 / (pred_norm * targ_norm)
        coef = inner * scale / (pred_norm * pred_norm)
        d_pred.append(
            (
                coef[:, None] * predicted[i] - scale[:, None] * targs[i].astype(jnp.float32)
            ).astype(jnp.bfloat16)
        )

    up = down_ = None
    sent = d_pred[0]
    for step in range(4):
        grads = [after(d_pred[0], sent), d_pred[1]]
        if up is None:
            sent = grad_block(table, acts, grads, 4, jnp.bfloat16)
        else:
            part = grad_block(table, acts, grads, 4 - step)
            sent = (part + up.astype(jnp.float32)).astype(jnp.bfloat16)
        up = shift(sent, "z", 1)
        if step < 3:
            grads = [after(d_pred[0], sent), d_pred[1]]
            if down_ is None:
                sent = grad_block(table, acts, grads, -3, jnp.bfloat16)
            else:
                part = grad_block(table, acts, grads, step - 3)
                sent = (part + down_.astype(jnp.float32)).astype(jnp.bfloat16)
            down_ = shift(sent, "z", -1)
    own = grad_block(table, acts, [after(d_pred[0], sent), d_pred[1]], 0)
    own = (own + down_.astype(jnp.float32) + up.astype(jnp.float32)).astype(jnp.bfloat16)
    full = assemble(table, lax.optimization_barrier((pair, right, left, *far, own))[:5])
    downs = [full, swap(full, "core")]
    grad = own.astype(jnp.float32) + swap(own, "yh").astype(jnp.float32)

    pieces = zip(jnp.split(state, 3, 0), jnp.split(other_state, 3, 0))
    new_rows = adam_step(*(ordered(a, b, yh, 0) for a, b in pieces), grad)
    block = new_rows.astype(jnp.bfloat16)
    rows_mine, rows_theirs = halves(halves(new_rows, yh, 0)[0], core, 0)
    new_map = ordered(rows_mine, swap(rows_theirs, "core"), core, 1)

    *joined, _ = ring_multiply(table, block, downs, dtype=jnp.bfloat16)
    joined = ordered(joined[0], swap(joined[1], "core"), core, 1)
    return (new_map, joined)


def solution(mesh):
    split = Mesh(mesh.devices.reshape(2, 8, 2, 4, 2), ("yh", "z", "core", "x", "yl"))
    return jax.shard_map(
        per_device,
        mesh=split,
        in_specs=(P(TOK, None), P(TOK, COL), P(TOK, COL), P(TOK, COL), P(TOK, COL), P(TOK, COL)),
        out_specs=(P(TOK, COL), P(TOK, COL)),
        check_vma=False,
    )
```

```python
import functools

import jax
import jax.numpy as jnp
from jax import lax
from jax.experimental import pallas as pl
from jax.experimental.pallas import tpu as pltpu
from jax.sharding import Mesh
from jax.sharding import PartitionSpec as P

COL = ("x", "yl")
TOK = ("yh", "z", "core")
NZ = 8
HALF = 256
VMEM_LIMIT = 2 * 2**20
SWAP = [(0, 1), (1, 0)]


def swap(x, axis):
    return lax.ppermute(x, axis, SWAP)


def shift(x, axis, by):
    n = lax.axis_size(axis)
    return lax.ppermute(x, axis, [(i, (i + by) % n) for i in range(n)])


def after(x, *deps):
    return lax.optimization_barrier((x, *deps))[0]


def halves(x, index, axis):
    first, second = jnp.split(x, 2, axis)
    return jnp.where(index, second, first), jnp.where(index, first, second)


def ordered(mine, theirs, index, axis):
    first = jnp.where(index, theirs, mine)
    second = jnp.where(index, mine, theirs)
    return jnp.concatenate([first, second], axis)


def multiply_kernel(offsets, summed, rowsums, tile, table, *refs):
    refs = list(refs)
    count = len(offsets)
    mats = [refs.pop(0) for _ in range(2)]
    blocks = [refs.pop(0) for _ in range(count)]
    sums = [refs.pop(0) for _ in range(2)] if summed else None
    targets = [refs.pop(0) for _ in range(2)] if rowsums else None
    outs = [refs.pop(0) for _ in range(2)]

    def step(s, carry):
        at = pl.ds(pl.multiple_of(s * tile, tile), tile)
        rows = []
        for i in range(2):
            total = sums[i][at, :] if summed else None
            for b in range(count):
                for h in range(2):
                    column = pl.multiple_of((h * NZ + table[offsets[b]]) * 256, 256)
                    part = jnp.dot(
                        mats[i][at, pl.ds(column, 256)],
                        blocks[b][h * 256 : h * 256 + 256, :],
                        preferred_element_type=jnp.float32,
                    )
                    total = part if total is None else total + part
            outs[i][at, :] = total.astype(outs[i].dtype)
            if rowsums:
                target = targets[i][at, :].astype(jnp.float32)
                rows += [
                    jnp.sum(value, axis=1, keepdims=True)
                    for value in (total * target, total * total, target * target)
                ]
        if rowsums:
            shape = (tile, 128)
            place = lax.broadcasted_iota(jnp.int32, shape, 1)
            result = jnp.zeros(shape, jnp.float32)
            for lane, row in zip((0, 1, 2, 4, 5, 6), rows):
                result = jnp.where(place == lane, row, result)
            refs[0][:, at] = result.T[:8]
        return carry

    lax.fori_loop(0, outs[0].shape[0] // tile, step, 0)


def load_kernel(source, target, sem):
    copy = pltpu.make_async_copy(source, target, sem)
    copy.start()
    copy.wait()


def load(x):
    return pl.pallas_call(
        load_kernel,
        in_specs=[pl.BlockSpec(memory_space=pltpu.HBM)],
        out_specs=pl.BlockSpec(memory_space=pltpu.VMEM),
        out_shape=jax.ShapeDtypeStruct(x.shape, x.dtype),
        scratch_shapes=[pltpu.SemaphoreType.DMA],
        compiler_params=pltpu.CompilerParams(vmem_limit_bytes=VMEM_LIMIT),
        name="load",
    )(x)


def assemble_kernel(table, *refs):
    parts, target, sems = refs[:4], refs[4], refs[5]
    copies = []
    for at, by in enumerate((0, 3, 1, 2)):
        column = pl.multiple_of((table[NZ] + by) % 4 * 1024, 1024)
        copies.append(
            pltpu.make_async_copy(parts[at], target.at[:, pl.ds(column, 1024)], sems.at[at])
        )
    for copy in copies:
        copy.start()
    for copy in copies:
        copy.wait()


def assemble(table, parts):
    return pl.pallas_call(
        assemble_kernel,
        in_specs=[pl.BlockSpec(memory_space=pltpu.SMEM)]
        + [pl.BlockSpec(memory_space=pltpu.HBM)] * 4,
        out_specs=pl.BlockSpec(memory_space=pltpu.VMEM),
        out_shape=jax.ShapeDtypeStruct((parts[0].shape[0], 4096), parts[0].dtype),
        scratch_shapes=[pltpu.SemaphoreType.DMA((4,))],
        compiler_params=pltpu.CompilerParams(vmem_limit_bytes=5 * VMEM_LIMIT),
        name="assemble",
    )(table, *parts)


def in_vmem(count):
    return [pl.BlockSpec(memory_space=pltpu.VMEM)] * count


def multiply(table, mats, blocks, offsets, sums=None, targets=None, dtype=jnp.float32):
    m = mats[0].shape[0]
    tile = 256 if m % 256 == 0 else 224
    count = len(blocks)
    args = [*mats, *blocks, *(sums or []), *(targets or [])]
    out_shape = [jax.ShapeDtypeStruct((m, HALF), dtype)] * 2
    if targets is not None:
        out_shape = out_shape + [jax.ShapeDtypeStruct((8, m), jnp.float32)]
    return pl.pallas_call(
        functools.partial(
            multiply_kernel, offsets, sums is not None, targets is not None, tile
        ),
        in_specs=[pl.BlockSpec(memory_space=pltpu.SMEM)] + in_vmem(len(args)),
        out_specs=in_vmem(len(out_shape)),
        out_shape=out_shape,
        compiler_params=pltpu.CompilerParams(
            vmem_limit_bytes=VMEM_LIMIT if m == 1024 else 5 * VMEM_LIMIT
        ),
        cost_estimate=pl.CostEstimate(
            flops=4 * m * HALF * 512 * count,
            bytes_accessed=4 * m * 512 * count + 8 * m * HALF,
            transcendentals=0,
        ),
        name=f"multiply_{m}_{count}",
    )(table, *args)


def grad_kernel(offset, table, *refs):
    mats, grads, out = refs[0:2], refs[2:4], refs[4]

    def step(h, carry):
        column = pl.multiple_of((h * NZ + table[offset]) * 256, 256)
        part = None
        for i in range(2):
            p = lax.dot_general(
                mats[i][:, pl.ds(column, 256)],
                grads[i][...],
                (((0,), (0,)), ((), ())),
                preferred_element_type=jnp.float32,
            )
            part = p if part is None else part + p
        out[pl.ds(pl.multiple_of(h * 256, 256), 256), :] = part.astype(out.dtype)
        return carry

    lax.fori_loop(0, 2, step, 0)


def grad_block(table, mats, grads, offset, dtype=jnp.float32):
    m = mats[0].shape[0]
    return pl.pallas_call(
        functools.partial(grad_kernel, offset % NZ),
        in_specs=[pl.BlockSpec(memory_space=pltpu.SMEM)] + in_vmem(4),
        out_specs=pl.BlockSpec(memory_space=pltpu.VMEM),
        out_shape=jax.ShapeDtypeStruct((512, HALF), dtype),
        compiler_params=pltpu.CompilerParams(vmem_limit_bytes=VMEM_LIMIT),
        cost_estimate=pl.CostEstimate(
            flops=4 * m * HALF * 512, bytes_accessed=4 * m * 512, transcendentals=0
        ),
        name="grad_block",
    )(table, *mats, *grads)


def ring_multiply(table, block, mats, targets=None, dtype=jnp.float32, early=None, later=None):
    up = down = block
    sums = None
    ready = [(block, 0)]
    for step in range(4):
        if sums is not None:
            up, sums = lax.optimization_barrier((up, sums))
        if step == 3 and early is not None:
            up, early = lax.optimization_barrier((up, early))
        if step > 0:
            ready += [(up, NZ - step), (down, step)]
        up = shift(up, "z", 1)
        if step < 3:
            down = shift(down, "z", -1)
        if step > 0:
            blocks, offsets = zip(*ready)
            sums = list(multiply(table, mats, blocks, offsets, sums))
            ready = []
    if later is not None:
        up, later = lax.optimization_barrier((up, later))
    return multiply(table, mats, [up], [4], sums, targets, dtype), early, later


def adam_step(weight, first, second, grad):
    moment1 = 0.9 * first + 0.1 * grad
    moment2 = 0.95 * second + 0.05 * grad * grad
    return weight - 0.02 * (moment1 / (1.0 - 0.9**10)) / (
        jnp.sqrt(moment2 / (1.0 - 0.95**10)) + 1e-08
    )


def per_device(activations, targets, map_weight, first_moment, second_moment, down_weight):
    core, yh, yl = (lax.axis_index(a) == 1 for a in ("core", "yh", "yl"))
    z = lax.axis_index("z").astype(jnp.int32)
    x = lax.axis_index("x").astype(jnp.int32)
    steps = lax.iota(jnp.int32, NZ + 1)
    table = jnp.where(steps < NZ, jnp.bitwise_and(z + steps, NZ - 1), x)

    map_half, yh, yl, table = lax.optimization_barrier(
        (map_weight.astype(jnp.bfloat16), yh, yl, table)
    )
    mine, theirs = halves(map_half, core, 1)
    chip_map = ordered(mine, swap(theirs, "core"), core, 0)
    other_map = swap(chip_map, "yh")
    block = ordered(chip_map, other_map, yh, 0)

    state = jnp.concatenate([map_weight, first_moment, second_moment], 0)
    mine, theirs = halves(after(state, chip_map), core, 1)
    theirs = swap(theirs, "core")
    pieces = zip(jnp.split(mine, 3, 0), jnp.split(theirs, 3, 0))
    state = jnp.concatenate([ordered(a, b, core, 0) for a, b in pieces], 0)
    other_state = swap(after(state, other_map), "yh")

    partner = swap(after(activations, chip_map, theirs), "core")
    acts = [activations, load(partner)]
    mine, theirs = halves(after(targets, other_map), core, 1)
    targs = [mine, swap(theirs, "core")]

    down = after(down_weight, other_map)
    pair = ordered(down, swap(down, "yl"), yl, 1)

    (*predicted, total), pair, other_state = ring_multiply(
        table, block, acts, targs, early=pair, later=other_state
    )
    theirs = swap(total, "core")
    total = total + jnp.concatenate([theirs[4:], theirs[:4]], 0)
    total = total + swap(total, "yl")
    total = total + lax.ppermute(total, "x", [(0, 1), (1, 0), (2, 3), (3, 2)])
    total = total + shift(total, "x", 2)
    d_pred = []
    for i in range(2):
        inner, pred_sq, target_sq = total[4 * i], total[4 * i + 1], total[4 * i + 2]
        pred_norm = jnp.sqrt(pred_sq + 1e-06)
        targ_norm = jnp.sqrt(target_sq + 1e-06)
        scale = 1.0 / (pred_norm * targ_norm)
        coef = inner * scale / (pred_norm * pred_norm)
        d_pred.append(
            (
                coef[:, None] * predicted[i] - scale[:, None] * targs[i].astype(jnp.float32)
            ).astype(jnp.bfloat16)
        )

    up = down_ = None
    sent = d_pred[0]
    for step in range(4):
        grads = [after(d_pred[0], sent), d_pred[1]]
        if up is None:
            sent = grad_block(table, acts, grads, 4, jnp.bfloat16)
        else:
            part = grad_block(table, acts, grads, 4 - step)
            sent = (part + up.astype(jnp.float32)).astype(jnp.bfloat16)
        up = shift(sent, "z", 1)
        if step < 3:
            grads = [after(d_pred[0], sent), d_pred[1]]
            if down_ is None:
                sent = grad_block(table, acts, grads, -3, jnp.bfloat16)
            else:
                part = grad_block(table, acts, grads, step - 3)
                sent = (part + down_.astype(jnp.float32)).astype(jnp.bfloat16)
            down_ = shift(sent, "z", -1)
        if step == 0:
            pair = after(pair, sent)
            right, left = shift(pair, "x", 1), shift(pair, "x", -1)
        if step == 1:
            opposite = shift(after(pair, sent), "x", 2)
    own = grad_block(table, acts, [after(d_pred[0], sent), d_pred[1]], 0)
    own = (own + down_.astype(jnp.float32) + up.astype(jnp.float32)).astype(jnp.bfloat16)
    other = swap(own, "yh")
    parts = lax.optimization_barrier((pair, right, left, opposite, other))[:4]
    full = assemble(table, parts)
    downs = [full, swap(full, "core")]
    grad = own.astype(jnp.float32) + other.astype(jnp.float32)

    pieces = zip(jnp.split(state, 3, 0), jnp.split(other_state, 3, 0))
    new_rows = adam_step(*(ordered(a, b, yh, 0) for a, b in pieces), grad)
    block = new_rows.astype(jnp.bfloat16)
    rows_mine, rows_theirs = halves(halves(new_rows, yh, 0)[0], core, 0)
    new_map = ordered(rows_mine, swap(rows_theirs, "core"), core, 1)

    joined, _, _ = ring_multiply(table, block, downs, dtype=jnp.bfloat16)
    joined = ordered(joined[0], swap(joined[1], "core"), core, 1)
    return (new_map, joined)


def solution(mesh):
    split = Mesh(mesh.devices.reshape(2, 8, 2, 4, 2), ("yh", "z", "core", "x", "yl"))
    return jax.shard_map(
        per_device,
        mesh=split,
        in_specs=(P(TOK, None), P(TOK, COL), P(TOK, COL), P(TOK, COL), P(TOK, COL), P(TOK, COL)),
        out_specs=(P(TOK, COL), P(TOK, COL)),
        check_vma=False,
    )
```

```python
import functools

import jax
import jax.numpy as jnp
from jax import lax
from jax.experimental import pallas as pl
from jax.experimental.pallas import tpu as pltpu
from jax.sharding import Mesh
from jax.sharding import PartitionSpec as P

COL = ("x", "yl")
TOK = ("yh", "z", "core")
NZ = 8
HALF = 256
VMEM_LIMIT = 2 * 2**20
SWAP = [(0, 1), (1, 0)]


def swap(x, axis):
    return lax.ppermute(x, axis, SWAP)


def shift(x, axis, by):
    n = lax.axis_size(axis)
    return lax.ppermute(x, axis, [(i, (i + by) % n) for i in range(n)])


def after(x, *deps):
    return lax.optimization_barrier((x, *deps))[0]


def halves(x, index, axis):
    first, second = jnp.split(x, 2, axis)
    return jnp.where(index, second, first), jnp.where(index, first, second)


def ordered(mine, theirs, index, axis):
    first = jnp.where(index, theirs, mine)
    second = jnp.where(index, mine, theirs)
    return jnp.concatenate([first, second], axis)


def multiply_kernel(offsets, summed, rowsums, tile, table, *refs):
    refs = list(refs)
    count = len(offsets)
    mats = [refs.pop(0) for _ in range(2)]
    blocks = [refs.pop(0) for _ in range(count)]
    sums = [refs.pop(0) for _ in range(2)] if summed else None
    targets = [refs.pop(0) for _ in range(2)] if rowsums else None
    outs = [refs.pop(0) for _ in range(2)]

    def step(s, carry):
        at = pl.ds(pl.multiple_of(s * tile, tile), tile)
        rows = []
        for i in range(2):
            total = sums[i][at, :] if summed else None
            for b in range(count):
                for h in range(2):
                    column = pl.multiple_of((h * NZ + table[offsets[b]]) * 256, 256)
                    part = jnp.dot(
                        mats[i][at, pl.ds(column, 256)],
                        blocks[b][h * 256 : h * 256 + 256, :],
                        preferred_element_type=jnp.float32,
                    )
                    total = part if total is None else total + part
            outs[i][at, :] = total.astype(outs[i].dtype)
            if rowsums:
                target = targets[i][at, :].astype(jnp.float32)
                rows += [
                    jnp.sum(value, axis=1, keepdims=True)
                    for value in (total * target, total * total, target * target)
                ]
        if rowsums:
            shape = (tile, 128)
            place = lax.broadcasted_iota(jnp.int32, shape, 1)
            result = jnp.zeros(shape, jnp.float32)
            for lane, row in zip((0, 1, 2, 4, 5, 6), rows):
                result = jnp.where(place == lane, row, result)
            refs[0][:, at] = result.T[:8]
        return carry

    lax.fori_loop(0, outs[0].shape[0] // tile, step, 0)


def load_kernel(source, target, sem):
    copy = pltpu.make_async_copy(source, target, sem)
    copy.start()
    copy.wait()


def load(x):
    return pl.pallas_call(
        load_kernel,
        in_specs=[pl.BlockSpec(memory_space=pltpu.HBM)],
        out_specs=pl.BlockSpec(memory_space=pltpu.VMEM),
        out_shape=jax.ShapeDtypeStruct(x.shape, x.dtype),
        scratch_shapes=[pltpu.SemaphoreType.DMA],
        compiler_params=pltpu.CompilerParams(vmem_limit_bytes=VMEM_LIMIT),
        name="load",
    )(x)


def assemble_kernel(table, *refs):
    parts, target, sems = refs[:4], refs[4], refs[5]
    copies = []
    for at, by in enumerate((0, 3, 1, 2)):
        column = pl.multiple_of((table[NZ] + by) % 4 * 1024, 1024)
        copies.append(
            pltpu.make_async_copy(parts[at], target.at[:, pl.ds(column, 1024)], sems.at[at])
        )
    for copy in copies:
        copy.start()
    for copy in copies:
        copy.wait()


def assemble(table, parts):
    return pl.pallas_call(
        assemble_kernel,
        in_specs=[pl.BlockSpec(memory_space=pltpu.SMEM)]
        + [pl.BlockSpec(memory_space=pltpu.HBM)] * 4,
        out_specs=pl.BlockSpec(memory_space=pltpu.VMEM),
        out_shape=jax.ShapeDtypeStruct((parts[0].shape[0], 4096), parts[0].dtype),
        scratch_shapes=[pltpu.SemaphoreType.DMA((4,))],
        compiler_params=pltpu.CompilerParams(vmem_limit_bytes=5 * VMEM_LIMIT),
        name="assemble",
    )(table, *parts)


def in_vmem(count):
    return [pl.BlockSpec(memory_space=pltpu.VMEM)] * count


def multiply(table, mats, blocks, offsets, sums=None, targets=None, dtype=jnp.float32):
    m = mats[0].shape[0]
    tile = 256 if m % 256 == 0 else 224
    count = len(blocks)
    args = [*mats, *blocks, *(sums or []), *(targets or [])]
    out_shape = [jax.ShapeDtypeStruct((m, HALF), dtype)] * 2
    if targets is not None:
        out_shape = out_shape + [jax.ShapeDtypeStruct((8, m), jnp.float32)]
    return pl.pallas_call(
        functools.partial(
            multiply_kernel, offsets, sums is not None, targets is not None, tile
        ),
        in_specs=[pl.BlockSpec(memory_space=pltpu.SMEM)] + in_vmem(len(args)),
        out_specs=in_vmem(len(out_shape)),
        out_shape=out_shape,
        compiler_params=pltpu.CompilerParams(
            vmem_limit_bytes=VMEM_LIMIT if m == 1024 else 5 * VMEM_LIMIT
        ),
        cost_estimate=pl.CostEstimate(
            flops=4 * m * HALF * 512 * count,
            bytes_accessed=4 * m * 512 * count + 8 * m * HALF,
            transcendentals=0,
        ),
        name=f"multiply_{m}_{count}",
    )(table, *args)


def grad_kernel(offset, table, *refs):
    mats, grads, out = refs[0:2], refs[2:4], refs[4]

    def step(h, carry):
        column = pl.multiple_of((h * NZ + table[offset]) * 256, 256)
        part = None
        for i in range(2):
            p = lax.dot_general(
                mats[i][:, pl.ds(column, 256)],
                grads[i][...],
                (((0,), (0,)), ((), ())),
                preferred_element_type=jnp.float32,
            )
            part = p if part is None else part + p
        out[pl.ds(pl.multiple_of(h * 256, 256), 256), :] = part.astype(out.dtype)
        return carry

    lax.fori_loop(0, 2, step, 0, unroll=offset in (4, 5, 3, 6))


def grad_block(table, mats, grads, offset, dtype=jnp.float32):
    m = mats[0].shape[0]
    return pl.pallas_call(
        functools.partial(grad_kernel, offset % NZ),
        in_specs=[pl.BlockSpec(memory_space=pltpu.SMEM)] + in_vmem(4),
        out_specs=pl.BlockSpec(memory_space=pltpu.VMEM),
        out_shape=jax.ShapeDtypeStruct((512, HALF), dtype),
        compiler_params=pltpu.CompilerParams(vmem_limit_bytes=VMEM_LIMIT),
        cost_estimate=pl.CostEstimate(
            flops=4 * m * HALF * 512, bytes_accessed=4 * m * 512, transcendentals=0
        ),
        name="grad_block",
    )(table, *mats, *grads)


def ring_multiply(table, block, mats, targets=None, dtype=jnp.float32, early=None, later=None):
    up = down = block
    sums = None
    ready = [(block, 0)]
    for step in range(4):
        if sums is not None:
            up, sums = lax.optimization_barrier((up, sums))
        if step == 3 and early is not None:
            up, early = lax.optimization_barrier((up, early))
        if step > 0:
            ready += [(up, NZ - step), (down, step)]
        up = shift(up, "z", 1)
        if step < 3:
            down = shift(down, "z", -1)
        if step > 0:
            blocks, offsets = zip(*ready)
            sums = list(multiply(table, mats, blocks, offsets, sums))
            ready = []
    if later is not None:
        up, later = lax.optimization_barrier((up, later))
    return multiply(table, mats, [up], [4], sums, targets, dtype), early, later


def adam_step(weight, first, second, grad):
    moment1 = 0.9 * first + 0.1 * grad
    moment2 = 0.95 * second + 0.05 * grad * grad
    return weight - 0.02 * (moment1 / (1.0 - 0.9**10)) / (
        jnp.sqrt(moment2 / (1.0 - 0.95**10)) + 1e-08
    )


def per_device(activations, targets, map_weight, first_moment, second_moment, down_weight):
    core, yh, yl = (lax.axis_index(a) == 1 for a in ("core", "yh", "yl"))
    z = lax.axis_index("z").astype(jnp.int32)
    x = lax.axis_index("x").astype(jnp.int32)
    steps = lax.iota(jnp.int32, NZ + 1)
    table = jnp.where(steps < NZ, jnp.bitwise_and(z + steps, NZ - 1), x)

    map_half, yh, yl, table = lax.optimization_barrier(
        (map_weight.astype(jnp.bfloat16), yh, yl, table)
    )
    mine, theirs = halves(map_half, core, 1)
    chip_map = ordered(mine, swap(theirs, "core"), core, 0)
    other_map = swap(chip_map, "yh")
    block = ordered(chip_map, other_map, yh, 0)

    state = jnp.concatenate([map_weight, first_moment, second_moment], 0)
    mine, theirs = halves(after(state, chip_map), core, 1)
    theirs = swap(theirs, "core")
    pieces = zip(jnp.split(mine, 3, 0), jnp.split(theirs, 3, 0))
    state = jnp.concatenate([ordered(a, b, core, 0) for a, b in pieces], 0)
    other_state = swap(after(state, other_map), "yh")

    partner = swap(after(activations, chip_map, theirs), "core")
    acts = [activations, load(partner)]
    mine, theirs = halves(after(targets, other_map), core, 1)
    targs = [mine, swap(theirs, "core")]

    down = after(down_weight, other_map)
    pair = ordered(down, swap(down, "yl"), yl, 1)

    (*predicted, total), pair, other_state = ring_multiply(
        table, block, acts, targs, early=pair, later=other_state
    )
    theirs = swap(total, "core")
    total = total + jnp.concatenate([theirs[4:], theirs[:4]], 0)
    total = total + swap(total, "yl")
    total = total + lax.ppermute(total, "x", [(0, 1), (1, 0), (2, 3), (3, 2)])
    total = total + shift(total, "x", 2)
    d_pred = []
    for i in range(2):
        inner, pred_sq, target_sq = total[4 * i], total[4 * i + 1], total[4 * i + 2]
        pred_norm = jnp.sqrt(pred_sq + 1e-06)
        targ_norm = jnp.sqrt(target_sq + 1e-06)
        scale = 1.0 / (pred_norm * targ_norm)
        coef = inner * scale / (pred_norm * pred_norm)
        d_pred.append(
            (
                coef[:, None] * predicted[i] - scale[:, None] * targs[i].astype(jnp.float32)
            ).astype(jnp.bfloat16)
        )

    up = down_ = None
    sent = d_pred[0]
    for step in range(4):
        grads = [after(d_pred[0], sent), d_pred[1]]
        if up is None:
            sent = grad_block(table, acts, grads, 4, jnp.bfloat16)
        else:
            part = grad_block(table, acts, grads, 4 - step)
            sent = (part + up.astype(jnp.float32)).astype(jnp.bfloat16)
        up = shift(sent, "z", 1)
        if step < 3:
            grads = [after(d_pred[0], sent), d_pred[1]]
            if down_ is None:
                sent = grad_block(table, acts, grads, -3, jnp.bfloat16)
            else:
                part = grad_block(table, acts, grads, step - 3)
                sent = (part + down_.astype(jnp.float32)).astype(jnp.bfloat16)
            down_ = shift(sent, "z", -1)
        if step == 0:
            pair = after(pair, sent)
            right, left = shift(pair, "x", 1), shift(pair, "x", -1)
        if step == 1:
            opposite = shift(after(pair, sent), "x", 2)
    own = grad_block(table, acts, [after(d_pred[0], sent), d_pred[1]], 0)
    own = (own + down_.astype(jnp.float32) + up.astype(jnp.float32)).astype(jnp.bfloat16)
    other = swap(own, "yh")
    parts = lax.optimization_barrier((pair, right, left, opposite, other))[:4]
    full = assemble(table, parts)
    downs = [full, swap(full, "core")]
    grad = own.astype(jnp.float32) + other.astype(jnp.float32)

    pieces = zip(jnp.split(state, 3, 0), jnp.split(other_state, 3, 0))
    new_rows = adam_step(*(ordered(a, b, yh, 0) for a, b in pieces), grad)
    block = new_rows.astype(jnp.bfloat16)
    rows_mine, rows_theirs = halves(halves(new_rows, yh, 0)[0], core, 0)
    new_map = ordered(rows_mine, swap(rows_theirs, "core"), core, 1)

    joined, _, _ = ring_multiply(table, block, downs, dtype=jnp.bfloat16)
    joined = ordered(joined[0], swap(joined[1], "core"), core, 1)
    return (new_map, joined)


def solution(mesh):
    split = Mesh(mesh.devices.reshape(2, 8, 2, 4, 2), ("yh", "z", "core", "x", "yl"))
    return jax.shard_map(
        per_device,
        mesh=split,
        in_specs=(P(TOK, None), P(TOK, COL), P(TOK, COL), P(TOK, COL), P(TOK, COL), P(TOK, COL)),
        out_specs=(P(TOK, COL), P(TOK, COL)),
        check_vma=False,
    )
```
